32 devices in a mesh: dp: 4 (over y, x), ctx: 8 (over z, core).
Axes of the slice: x: 2, y: 2, z: 4, core: 2. Of those that a mesh axis runs over, the one named last changes fastest.
Arguments:
- inputs: bfloat16 [4096, 8192], P(('dp', 'ctx')), may hold values from -6 to 6
- out_grad: bfloat16 [4096, 8192], P(('dp', 'ctx')), may hold values from -6 to 6
- b_matrix: bfloat16 [4096, 512], P(('dp', 'ctx')), may hold values from -6 to 6
- c_matrix: bfloat16 [4096, 512], P(('dp', 'ctx')), may hold values from -0.5 to 0.5
- step_raw: bfloat16 [4096, 128], P(('dp', 'ctx'))
- hidden: bfloat16 [4096, 8192], P(('dp', 'ctx')), may hold values from -6 to 6
- log_rates: float32 [128], replicated, may hold values from 0 to 0.6931
- step_bias: float32 [128], replicated
- skip_head_gain: float32 [128], replicated, may hold values from 0.1 to 0.6
- doc_lengths: int32 [4, 4], P('dp'), may hold values from 1 to 512, 1024 in all within a row
- counts: int32 [4], P('dp'), may hold values from 128 to 1024
Outputs:
- grad_inputs: bfloat16 [4096, 8192], P(('dp', 'ctx'))
- grad_b: bfloat16 [4096, 512], P(('dp', 'ctx'))
- grad_c: bfloat16 [4096, 512], P(('dp', 'ctx'))
- grad_steps: bfloat16 [4096, 128], P(('dp', 'ctx'))
- grad_weight: float32 [8192, 128], P(('dp', 'ctx'))
The draws below stay inside these ranges and needn't reach their ends.
Inputs may be any that keep to these rules, and one draw needn't show every extreme that they name: `doc_lengths`: each sequence's 4 lengths sum to 1024; the longest is exactly 512.
All inputs are finite; a program needn't handle non-finite values.
Results may differ from the reference program's by a relative error of at most 0.0025.
Values may be sent and summed in bfloat16 or wider, within the bound.
No kernel may reach another device: no remote copies, remote signals or barrier semaphores. Data moves between devices by JAX's collectives and lax.ppermute only.
A program may use at most 128 MiB of HBM per device.

```python
import math
import jax
import jax.numpy as jnp
import numpy as np
from jax import lax

D = 8192
H = 128
P_SIZE = 64
N = 128
G = 4
BLOCK = 128
DOCS = 4
LARGE_STEP_TOKENS = 2
SEQUENCE_LENGTH = 1024
SEQUENCE_COUNT = 4
TOKENS_ALL = 4096


def draw_step_raw(key, part):
    noise_key, placement_key = jax.random.split(jax.random.fold_in(key, 11))
    noise = jnp.clip(0.5 * jax.random.normal(noise_key, (SEQUENCE_COUNT, SEQUENCE_LENGTH, H), jnp.float32), -1.5, 1.5)
    token_places = jax.random.randint(placement_key, (SEQUENCE_COUNT, LARGE_STEP_TOKENS), 0, SEQUENCE_LENGTH)
    marked = jnp.any(jnp.arange(SEQUENCE_LENGTH)[None, :, None] == token_places[:, None, :], axis=2)
    height = jnp.log(0.6 * SEQUENCE_LENGTH) * jnp.ones((), jnp.float32)
    values = jnp.where(marked[:, :, None], height, noise)
    return values.reshape(SEQUENCE_COUNT * SEQUENCE_LENGTH, H).astype(jnp.bfloat16)


def draw_step_bias(key, part):
    kind_key, size_key = jax.random.split(jax.random.fold_in(key, 23))
    slow_heads = jax.random.bernoulli(kind_key, 0.5, (H,))
    factor = jnp.exp(jax.random.uniform(size_key, (H,), jnp.float32, -0.35, 0.35))
    target = jnp.where(slow_heads, 0.4 / SEQUENCE_LENGTH, 0.017) * factor
    return jnp.log(jnp.expm1(target))


def place_ends(values, rng, least, high):
    extent = values.shape
    spot = [jax.random.randint(jax.random.fold_in(rng, axis), (), 0, extent[axis]) for axis in range(len(extent))]
    values = values.at[tuple(spot)].set(least)
    longest = extent.index(max(extent))
    spot[longest] = (spot[longest] + 1) % extent[longest]
    return values.at[tuple(spot)].set(high)


def raised(values, stream_key, source, target, parts, factor):
    def block_of(axis_at):
        return (jnp.arange(values.shape[axis_at]) // (values.shape[axis_at] // parts)).reshape((-1,) + (1,) * (values.ndim - 1 - axis_at))

    one_side = jax.random.permutation(stream_key, parts)[block_of(target)]
    far = (block_of(target) + parts // 2) % parts
    return jnp.where((block_of(source) == one_side) | (block_of(source) == far), factor * values, values)


def steps_of(stream_key, dims, cuts, least, largest):
    gain = 1.0
    for dim, blocks in cuts:
        heights = jax.random.uniform(jax.random.fold_in(jax.random.fold_in(stream_key, 6), dim), (blocks,), jnp.float32, least / len(cuts), largest / len(cuts))
        gain = gain * jnp.repeat(jnp.exp(heights), dims[dim] // blocks).reshape((-1,) + (1,) * (len(dims) - 1 - dim))
    return gain


def length_profile(count, total, most, slope):
    loads = [(1 << 20) // math.isqrt(standing ** slope) + 1 for standing in range(2, count + 1)]
    spare, given = total - most - (count - 1), [1] * (count - 1)
    while spare > 0:
        free = [i for i in range(count - 1) if given[i] < most]
        whole, remaining = sum([loads[i] for i in free]), spare
        for i in free:
            more = min(most - given[i], max(1, remaining * loads[i] // whole), spare)
            given[i] = given[i] + more
            spare = spare - more
    return np.array([most] + given)


def ragged(stream_key, count, total, most, skew):
    if count == 2:
        one = jax.random.randint(stream_key, (), max(1, total - most), min(most, total - 1) + 1)
        return jnp.stack([one, total - one])
    sizes = jnp.asarray(length_profile(count, total, most, skew), jnp.int32)
    pairs = (count - 1) // 2
    giver, sink = sizes[1:1 + 2 * pairs:2], sizes[2:2 + 2 * pairs:2]
    margin = jnp.minimum(giver - 1, most - sink)
    moved = jax.random.randint(jax.random.fold_in(stream_key, 1), (pairs,), 0, 1 << 20) % (margin + 1)
    sizes = sizes.at[1:1 + 2 * pairs:2].set(giver - moved).at[2:2 + 2 * pairs:2].set(sink + moved)
    return sizes[jax.random.permutation(jax.random.fold_in(stream_key, 2), count)]


def normal_values(rng, shape, width, limit, cuts=(), kind=jnp.bfloat16):
    values = jax.random.normal(rng, shape, jnp.float32) * width
    if len(cuts) > 0:
        values = steps_of(rng, shape, cuts, -0.22, 0.18) * values
    return jnp.clip(values, min=-limit, max=limit).astype(kind)


def noise_with(stream_key, extent, spread, reach, cuts, heavy, kind=jnp.bfloat16):
    result = spread * jax.random.normal(stream_key, extent, jnp.float32)
    if cuts:
        result = result * steps_of(stream_key, extent, cuts, -0.22, 0.18)
    return jnp.clip(raised(result, jax.random.fold_in(stream_key, 3), *heavy), -reach, reach).astype(kind)


def setup_inputs(seed: int = 0) -> dict:
    streams_of = jax.random.split(jax.random.key(seed), 12)
    inputs = normal_values(streams_of[0], (TOKENS_ALL, H * P_SIZE), 1.0, 6.0, ((0, 32),))
    out_grad = normal_values(streams_of[1], (TOKENS_ALL, H * P_SIZE), 1.0, 6.0, ((0, 32),))
    b_matrix = normal_values(streams_of[2], (TOKENS_ALL, G * N), 1.0, 6.0, ((0, 32),))
    c_matrix = normal_values(streams_of[3], (TOKENS_ALL, G * N), N ** -0.5, 0.5, ((0, 32),))
    step_raw = draw_step_raw(jax.random.fold_in(streams_of[11], 71), 0)
    hidden = noise_with(streams_of[5], (TOKENS_ALL, D), 1.0, 6.0, ((0, 32),), (0, 1, 32, 2.75))
    log_rates = jnp.clip(jax.random.uniform(streams_of[6], (H,), jnp.float32, 0.0, 0.6931), 0.0, 0.6931)
    step_bias = draw_step_bias(jax.random.fold_in(streams_of[11], 71), 0)
    skip_head_gain = jnp.clip(jax.random.uniform(streams_of[8], (H,), jnp.float32, 0.1, 0.6), 0.1, 0.6)
    doc_lengths = jax.vmap(lambda own: ragged(own, DOCS, SEQUENCE_LENGTH, SEQUENCE_LENGTH // 2, 0))(jax.random.split(streams_of[9], SEQUENCE_COUNT)).reshape((SEQUENCE_COUNT, DOCS)).astype(jnp.int32)
    counts = place_ends(jax.random.randint(streams_of[10], (SEQUENCE_COUNT,), SEQUENCE_LENGTH // 8, SEQUENCE_LENGTH + 1), jax.random.fold_in(streams_of[10], 1), SEQUENCE_LENGTH // 8, SEQUENCE_LENGTH).astype(jnp.int32)
    return {"inputs": inputs, "out_grad": out_grad, "b_matrix": b_matrix, "c_matrix": c_matrix, "step_raw": step_raw, "hidden": hidden, "log_rates": log_rates, "step_bias": step_bias, "skip_head_gain": skip_head_gain, "doc_lengths": doc_lengths, "counts": counts}


HIGHEST = lax.Precision.HIGHEST

def split_blocks(tensor, block_width):
    return tensor.reshape((tensor.shape[0] // block_width, block_width) + tensor.shape[1:])

def decay_tables(log_decay, resets):
    length_q = log_decay.shape[0]
    summed = jnp.moveaxis(jnp.cumsum(log_decay, axis=0), 0, -1)
    segment = jnp.cumsum(resets)
    index_row = jnp.arange(length_q)
    allowed = (index_row[:, None] >= index_row[None, :]) & (segment[:, None] == segment[None, :])
    gap_log = summed[..., :, None] - summed[..., None, :]
    within = jnp.where(allowed, jnp.exp(jnp.minimum(gap_log, 0.0)), 0.0)
    before = jnp.where(segment == 0, jnp.exp(summed), 0.0)
    behind = jnp.where(segment == segment[-1], jnp.exp(summed[..., -1:] - summed), 0.0)
    return (within, before, behind)

def block_ends(values, cotangent, b_rows, c_rows, step_lanes, before, behind):
    b_wide = b_rows.astype(values.dtype)
    c_wide = c_rows.astype(values.dtype)
    state_ends = jnp.einsum('gkq,qgkp,qgn->gkpn', behind * step_lanes, values, b_wide, precision=HIGHEST)
    starts = jnp.einsum('gkq,qgkp,qgn->gkpn', before, cotangent, c_wide, precision=HIGHEST)
    return (state_ends, starts)

def block_grads(values, cotangent, b_rows, c_rows, step_lanes, sigmoid_t, tables, state_in, flow_in, skip_local, neg_rate):
    within, before, behind = tables
    b_wide = b_rows.astype(values.dtype)
    c_wide = c_rows.astype(values.dtype)
    length_q = values.shape[0]
    index_row = jnp.arange(length_q)
    upper_mask = (index_row[:, None] >= index_row[None, :]).astype(values.dtype)
    steps_q = jnp.moveaxis(step_lanes, -1, 0)
    before_q = jnp.moveaxis(before, -1, 0)
    behind_q = jnp.moveaxis(behind, -1, 0)
    cross_bc = jnp.einsum('tgn,sgn->gts', c_rows, b_rows, preferred_element_type=jnp.float32).astype(values.dtype)
    pair_dots = jnp.einsum('ugkp,sgkp->gkus', cotangent, values, precision=HIGHEST)
    weighted = within * step_lanes[..., None, :] * pair_dots
    coupled = within * cross_bc[:, None]
    flow_b = jnp.einsum('gkpn,sgn->sgkp', flow_in, b_wide, precision=HIGHEST)
    slope_term = jnp.einsum('gkus,ugkp->sgkp', coupled, cotangent, precision=HIGHEST) + behind_q[..., None] * flow_b
    grad_values = steps_q[..., None] * slope_term + skip_local[..., None] * cotangent
    values_flow = jnp.einsum('sgkp,gkpn->sgkn', values, flow_in, precision=HIGHEST)
    grad_b = jnp.einsum('gkus,ugn->sgn', weighted, c_wide, precision=HIGHEST) + jnp.einsum('sgk,sgkn->sgn', steps_q * behind_q, values_flow, precision=HIGHEST)
    grad_c = jnp.einsum('gkts,sgn->tgn', weighted, b_wide, precision=HIGHEST) + jnp.einsum('tgk,tgkp,gkpn->tgn', before_q, cotangent, state_in, precision=HIGHEST)
    state_c = jnp.einsum('gkpn,ugn->ugkp', state_in, c_wide, precision=HIGHEST)
    direct = lax.optimization_barrier(jnp.sum(values * slope_term, axis=-1))
    entering = before_q * lax.optimization_barrier(jnp.sum(cotangent * state_c, axis=-1))
    leaving = behind_q * steps_q * lax.optimization_barrier(jnp.sum(values * flow_b, axis=-1))
    products = weighted * cross_bc[:, None]
    crossing = jnp.cumsum(products, axis=-1) - products
    crossing_sum = jnp.moveaxis(lax.optimization_barrier(jnp.sum(crossing * upper_mask, axis=-2)), -1, 0)
    entering_sum = jnp.flip(jnp.cumsum(jnp.flip(entering, 0), axis=0), 0)
    leaving_sum = jnp.cumsum(leaving, axis=0) - leaving
    through = before[..., -1] * lax.optimization_barrier(jnp.sum(flow_in * state_in, axis=(-2, -1)))
    decay_grad = crossing_sum + entering_sum + leaving_sum + through
    grad_steps = (direct + neg_rate * decay_grad) * sigmoid_t
    return (grad_values, grad_b, grad_c, grad_steps)

def carry_forward(decays, state_ends, initial):

    def advance(carried, element):
        return (element[0][..., None, None] * carried + element[1], carried)
    last_carry, entering = lax.scan(advance, initial, (decays, state_ends))
    return (entering, last_carry)

def carry_backward(decays, starts, incoming):

    def retreat(carried, element):
        return (element[0][..., None, None] * carried + element[1], carried)
    first_carry, leaving = lax.scan(retreat, incoming, (decays, starts), reverse=True)
    return (leaving, first_carry)

def prepare_blocks(values, cotangent, b_rows, c_rows, step_sizes, sigmoid_t, resets, neg_rate, block_width):
    pieces = tuple((split_blocks(tensor, block_width) for tensor in (values, cotangent, b_rows, c_rows, step_sizes, sigmoid_t, resets)))
    tables = jax.vmap(decay_tables)(pieces[4] * neg_rate, pieces[6])
    step_lanes = jnp.moveaxis(pieces[4], 1, -1)
    state_ends, starts = jax.vmap(block_ends)(pieces[0], pieces[1], pieces[2], pieces[3], step_lanes, tables[1], tables[2])
    return (pieces, step_lanes, tables, state_ends, starts)

def finish_blocks(prepared, skip_local, neg_rate, state_in, flow_in):
    pieces, step_lanes, tables, state_ends, starts = prepared
    decays = tables[1][..., -1]
    entering = carry_forward(decays, state_ends, state_in)[0]
    leaving = carry_backward(decays, starts, flow_in)[0]

    def one_block(element):
        return block_grads(element[0], element[1], element[2], element[3], element[4], element[5], element[6], element[7], element[8], skip_local, neg_rate)
    results = lax.map(one_block, (pieces[0], pieces[1], pieces[2], pieces[3], step_lanes, pieces[5], tables, entering, leaving))
    return tuple((tensor.reshape((-1,) + tensor.shape[2:]) for tensor in results))

def reference(inputs, out_grad, b_matrix, c_matrix, step_raw, hidden, log_rates, step_bias, skip_head_gain, doc_lengths, counts):
    per_group = H // G
    count_f = counts.astype(jnp.float32)
    weights = count_f * SEQUENCE_COUNT / jnp.sum(count_f)
    neg_rate = (-jnp.exp(log_rates)).reshape(G, per_group)
    skip_local = skip_head_gain.reshape(G, per_group)
    positions = jnp.arange(SEQUENCE_LENGTH)

    def one_sequence(element):
        values, cotangent, b_rows, c_rows, raw_steps, lengths, weight = element
        values = values.astype(jnp.float32).reshape(SEQUENCE_LENGTH, G, per_group, P_SIZE)
        cotangent = cotangent.astype(jnp.float32).reshape(SEQUENCE_LENGTH, G, per_group, P_SIZE) * weight
        b_rows = b_rows.reshape(SEQUENCE_LENGTH, G, N)
        c_rows = c_rows.reshape(SEQUENCE_LENGTH, G, N)
        shifted = raw_steps.astype(jnp.float32) + step_bias
        step_sizes = jax.nn.softplus(shifted).reshape(SEQUENCE_LENGTH, G, per_group)
        sigmoid_t = jax.nn.sigmoid(shifted).reshape(SEQUENCE_LENGTH, G, per_group)
        starts_doc = jnp.cumsum(lengths) - lengths
        resets = jnp.any(positions[:, None] == starts_doc[None, :], axis=1).astype(jnp.float32)
        prepared = prepare_blocks(values, cotangent, b_rows, c_rows, step_sizes, sigmoid_t, resets, neg_rate, BLOCK)
        empty_state = jnp.zeros((G, per_group, P_SIZE, N), jnp.float32)
        grad_values, grad_b, grad_c, grad_steps = finish_blocks(prepared, skip_local, neg_rate, empty_state, empty_state)
        return (grad_values.reshape(SEQUENCE_LENGTH, H * P_SIZE).astype(jnp.bfloat16), grad_b.reshape(SEQUENCE_LENGTH, G * N).astype(jnp.bfloat16), grad_c.reshape(SEQUENCE_LENGTH, G * N).astype(jnp.bfloat16), grad_steps.reshape(SEQUENCE_LENGTH, H).astype(jnp.bfloat16))
    results = lax.map(one_sequence, (inputs.reshape(SEQUENCE_COUNT, SEQUENCE_LENGTH, H * P_SIZE), out_grad.reshape(SEQUENCE_COUNT, SEQUENCE_LENGTH, H * P_SIZE), b_matrix.reshape(SEQUENCE_COUNT, SEQUENCE_LENGTH, G * N), c_matrix.reshape(SEQUENCE_COUNT, SEQUENCE_LENGTH, G * N), step_raw.reshape(SEQUENCE_COUNT, SEQUENCE_LENGTH, H), doc_lengths, weights))
    grad_inputs = results[0].reshape(SEQUENCE_COUNT * SEQUENCE_LENGTH, H * P_SIZE)
    grad_b = results[1].reshape(SEQUENCE_COUNT * SEQUENCE_LENGTH, G * N)
    grad_c = results[2].reshape(SEQUENCE_COUNT * SEQUENCE_LENGTH, G * N)
    grad_steps = results[3].reshape(SEQUENCE_COUNT * SEQUENCE_LENGTH, H)
    grad_weight = jnp.dot(hidden.T, grad_steps, preferred_element_type=jnp.float32) * (1.0 / math.sqrt(SEQUENCE_COUNT * SEQUENCE_LENGTH))
    return (grad_inputs, grad_b, grad_c, grad_steps, grad_weight)
```

```python
import functools
import math

import jax
import jax.numpy as jnp
from jax import lax
from jax.experimental import pallas as pl
from jax.experimental.pallas import tpu as pltpu
from jax.sharding import PartitionSpec as P

HEAD = 64
N = 128
Q = 128
LANES = 128
WIDE1 = 1024
WIDE2 = 512
WIDE3 = 1024
CHUNKS = 2
F32 = jnp.float32
BF16 = jnp.bfloat16
HIGHEST = lax.Precision.HIGHEST


def split(value):
    high = value.astype(BF16)
    return high, (value - high.astype(F32)).astype(BF16)


def nn(a, b):
    return lax.dot_general(a, b, (((1,), (0,)), ((), ())), preferred_element_type=F32)


def nt(a, b):
    return lax.dot_general(a, b, (((1,), (1,)), ((), ())), preferred_element_type=F32)


def tn(a, b):
    return lax.dot_general(a, b, (((0,), (0,)), ((), ())), preferred_element_type=F32)


def iota(shape, axis):
    return lax.broadcasted_iota(jnp.int32, shape, axis)


def head_selector(first_head, width):
    shape = (LANES, width)
    return ((iota(shape, 1) // HEAD + first_head) == iota(shape, 0)).astype(F32).astype(BF16)


def forward_role(shape):
    return iota(shape, 0) < (lax.axis_index("ctx") % 2) * (1 << 20)


def prep_kernel(
    docs_ref, raw_ref, far_ref, rate_ref, bias_ref, skip_ref,
    whi_ref, wlo_ref, fhi_ref, flo_ref, col_ref, row_ref, mask_ref, khi_ref, klo_ref, ratio_ref, rate_out_ref, down_ref,
):
    ctx = lax.axis_index("ctx")
    core = ctx % 2
    square = (Q, Q)
    sub, lane = iota(square, 0), iota(square, 1)
    lower = (sub >= lane).astype(F32)
    neg = -jnp.exp(rate_ref[...])
    bias = bias_ref[...]
    starts, total = [], jnp.int32(0)
    for d in range(docs_ref.shape[1]):
        starts.append(total)
        total = total + docs_ref[0, d]

    def segments(base, index):
        seg, last = jnp.zeros(square, jnp.int32), jnp.int32(0)
        for start in starts:
            rel = jnp.where(start >= base, start - base, 1 << 20)
            seg = seg + (index >= rel).astype(jnp.int32)
            last = last + jnp.where(rel < Q, 1, 0)
        return seg, last

    def side(raw, base):
        shifted = raw.astype(F32) + bias
        step = jnp.maximum(shifted, 0.0) + jnp.log1p(jnp.exp(-jnp.abs(shifted)))
        summed = jnp.dot(lower, step * neg, precision=HIGHEST, preferred_element_type=F32)
        seg, last = segments(base, sub)
        before = jnp.where(seg == 0, jnp.exp(summed), 0.0)
        behind = jnp.where(seg == last, jnp.exp(summed[Q - 1 :, :] - summed), 0.0)
        return shifted, step, summed, seg, before, behind

    own_base, far_base = ctx * Q, (ctx + 1 - 2 * core) * Q
    shifted, step, summed, seg, before, behind = side(raw_ref[...], own_base)
    _, step_f, _, _, before_f, behind_f = side(far_ref[...], far_base)
    down, down_f = before[Q - 1 :, :], before_f[Q - 1 :, :]
    forward = forward_role(square)
    own = jnp.where(forward, behind * step, before)
    far = jnp.where(forward, behind_f * step_f, before_f)
    row = iota((16, LANES), 0)
    rows = jnp.where(row == 0, down_f, jnp.where(row == 1, down * down_f, jnp.where(row == 2, skip_ref[...], 0.0)))
    whi_ref[...], wlo_ref[...] = split(jnp.concatenate([own, far * down, rows], axis=0))
    fhi_ref[...], flo_ref[...] = split(far)
    col_ref[...] = summed - jnp.log(jnp.maximum(step, 1e-37))
    row_ref[...] = summed.T
    seg_u, _ = segments(own_base, lane)
    mask_ref[...] = jnp.where((lane >= sub) & (seg_u == seg), 0.0, -1e30)
    khi_ref[...], klo_ref[...] = split(jnp.concatenate([step * behind, before], axis=0))
    sigmoid = 1.0 / (1.0 + jnp.exp(-shifted))
    ratio_ref[...] = jnp.where(step < 1e-30, 1.0, sigmoid / jnp.maximum(step, 1e-30))
    rate_out_ref[...] = neg * sigmoid
    down_ref[...] = jnp.broadcast_to(down, (8, LANES))


def prep(docs, raw, far_small, rate, bias, skip, far_block):
    full = lambda shape: pl.BlockSpec(shape, lambda i: (0, 0))
    sq = jax.ShapeDtypeStruct((Q, LANES), F32)
    outs = [
        jax.ShapeDtypeStruct((2 * Q + 16, LANES), BF16),
        jax.ShapeDtypeStruct((2 * Q + 16, LANES), BF16),
        jax.ShapeDtypeStruct((Q, LANES), BF16),
        jax.ShapeDtypeStruct((Q, LANES), BF16),
        sq, sq, sq,
        jax.ShapeDtypeStruct((2 * Q, LANES), BF16),
        jax.ShapeDtypeStruct((2 * Q, LANES), BF16),
        sq, sq,
        jax.ShapeDtypeStruct((8, LANES), F32),
    ]
    return pl.pallas_call(
        prep_kernel,
        name="prep",
        grid=(1,),
        in_specs=[
            pl.BlockSpec(memory_space=pltpu.SMEM),
            full((Q, LANES)),
            pl.BlockSpec((Q, LANES), lambda i: (0, far_block)),
            full((1, LANES)), full((1, LANES)), full((1, LANES)),
        ],
        out_specs=[full(o.shape) for o in outs],
        out_shape=outs,
        cost_estimate=pl.CostEstimate(flops=20_000_000, transcendentals=200_000, bytes_accessed=1_000_000),
    )(docs, raw, far_small, rate, bias, skip)


def state_kernel(first, whi_ref, wlo_ref, x_ref, g_ref, far_ref, b_ref, c_ref, mf_ref, t_ref, rows_ref):
    i = pl.program_id(0)
    sel = head_selector((first + i) * (WIDE1 // HEAD), WIDE1)
    wide = nn(whi_ref[...], sel) + nn(wlo_ref[...], sel)
    forward = forward_role((Q, WIDE1))
    own = jnp.where(forward, x_ref[...].astype(F32), g_ref[...].astype(F32))
    scaled = jnp.concatenate([own * wide[:Q], far_ref[...].astype(F32) * wide[Q : 2 * Q]], axis=0)
    high, low = split(scaled)
    role = forward_role((Q, N))
    m_own = jnp.where(role, b_ref[...].astype(F32), c_ref[...].astype(F32))
    m = jnp.concatenate([m_own, mf_ref[...].astype(F32)], axis=0).T.astype(BF16)
    t_ref[...] = (nn(m, high) + nn(m, low)).astype(BF16)
    rows_ref[...] = wide[2 * Q :]


def chip_state(chunk, width, group_width, whi, wlo, x, g, far, b, c, far_small):
    steps = width // WIDE1
    first = chunk * steps
    group = lambda i: (first + i) * WIDE1 // group_width
    whole = lambda a: pl.BlockSpec(a.shape, lambda i: (0, 0))
    return pl.pallas_call(
        functools.partial(state_kernel, first),
        name="chip_state",
        grid=(steps,),
        in_specs=[
            whole(whi), whole(wlo),
            pl.BlockSpec((Q, WIDE1), lambda i: (0, first + i)),
            pl.BlockSpec((Q, WIDE1), lambda i: (0, first + i)),
            pl.BlockSpec((Q, WIDE1), lambda i: (0, i)),
            pl.BlockSpec((Q, N), lambda i: (0, group(i))),
            pl.BlockSpec((Q, N), lambda i: (0, group(i))),
            pl.BlockSpec((Q, N), lambda i: (0, group(i))),
        ],
        out_specs=[pl.BlockSpec((N, WIDE1), lambda i: (0, i)), pl.BlockSpec((16, WIDE1), lambda i: (0, i))],
        out_shape=[jax.ShapeDtypeStruct((N, width), BF16), jax.ShapeDtypeStruct((16, width), F32)],
        cost_estimate=pl.CostEstimate(flops=8 * N * 2 * Q * width, transcendentals=0, bytes_accessed=8 * Q * width),
    )(whi, wlo, x, g, far, b, c, far_small)


def block_kernel(
    first, per_group, fhi_ref, flo_ref, col_ref, row_ref, mask_ref, rows_ref, x_ref, g_ref, far_ref, b_ref, c_ref, mf_ref,
    p_ref, tf_ref, cc_ref, r_ref, gb_ref, gc_ref, cross_ref, w_ref, rt_ref,
):
    i = pl.program_id(0)
    heads = WIDE2 // HEAD
    block = first + i

    @pl.when(i == 0)
    def _():
        cc_ref[...] = jnp.zeros_like(cc_ref)
        rt_ref[...] = jnp.zeros_like(rt_ref)

    @pl.when(i % per_group == 0)
    def _():
        cross = nt(b_ref[...], c_ref[...])
        cross_ref[...] = jnp.concatenate([cross, cross], axis=1)
        w_ref[...] = jnp.zeros_like(w_ref)

    lane = iota((Q, LANES), 1)
    left = (lane < HEAD).astype(F32).astype(BF16)
    right = (lane >= HEAD).astype(F32).astype(BF16)
    mask = mask_ref[...]
    cross = cross_ref[...]
    cols = pltpu.roll(col_ref[...], (LANES - heads * block) % LANES, 1)
    srow = row_ref[pl.ds(pl.multiple_of(heads * block, 8), heads), :]
    skip = rows_ref[2:3, :]
    cc = jnp.zeros((Q, LANES), F32)
    wsum = w_ref[...]
    sums = []
    for j in range(heads // 2):
        at = slice(LANES * j, LANES * (j + 1))
        xp, gp = x_ref[:, at], g_ref[:, at]
        stacked = jnp.concatenate([gp * left, gp * right], axis=0)
        pair = nt(xp, stacked)
        gap = jnp.concatenate(
            [mask + (srow[k : k + 1, :] - cols[:, k : k + 1]) for k in (2 * j, 2 * j + 1)], axis=1
        )
        within = jnp.exp(gap)
        coupled = within * cross
        weighted = within * pair
        product = coupled * pair
        wsum = wsum + weighted
        high, low = split(coupled)
        p_ref[:, at] = nn(high, stacked) + nn(low, stacked) + skip[:, at] * gp.astype(F32)
        over = jnp.sum(product, axis=0, keepdims=True)
        sums += [over[:, :Q], over[:, Q:]]
        for k in (0, 1):
            column = jnp.sum(product[:, Q * k : Q * (k + 1)], axis=1, keepdims=True)
            cc = jnp.where(lane == heads * block + 2 * j + k, column, cc)
    cc_ref[...] += cc
    rt_ref[pl.ds(pl.multiple_of(heads * block, 8), heads), :] = jnp.concatenate(sums, axis=0)
    w_ref[...] = wsum

    sel = head_selector(block * heads, WIDE2)
    wide = nn(fhi_ref[...], sel) + nn(flo_ref[...], sel)
    high, low = split(far_ref[...].astype(F32) * wide)
    m = mf_ref[...].astype(F32).T.astype(BF16)
    tf_ref[...] = nn(m, high) + nn(m, low)

    @pl.when(i % per_group == per_group - 1)
    def _():
        folded = wsum[:, :Q] + wsum[:, Q:]
        high, low = split(folded)
        gb_ref[...] = nn(high, c_ref[...]) + nn(low, c_ref[...])
        high, low = split(folded.T)
        gc_ref[...] = nn(high, b_ref[...]) + nn(low, b_ref[...])

    @pl.when(i == pl.num_programs(0) - 1)
    def _():
        r_ref[...] = rt_ref[...].T


def within_block(chunk, width, group_width, fhi, flo, col, row, mask, rows, x, g, far, b, c, far_small):
    steps = width // WIDE2
    first = chunk * steps
    per_group = group_width // WIDE2
    whole = lambda a: pl.BlockSpec(a.shape, lambda i: (0, 0))
    group = pl.BlockSpec((Q, N), lambda i: (0, (first + i) // per_group))
    groups = width // group_width
    return pl.pallas_call(
        functools.partial(block_kernel, first, per_group),
        name="within_block",
        grid=(steps,),
        in_specs=[
            whole(fhi), whole(flo), whole(col), whole(row), whole(mask),
            pl.BlockSpec((16, WIDE2), lambda i: (0, i)),
            pl.BlockSpec((Q, WIDE2), lambda i: (0, first + i)),
            pl.BlockSpec((Q, WIDE2), lambda i: (0, first + i)),
            pl.BlockSpec((Q, WIDE2), lambda i: (0, i)),
            group, group, group,
        ],
        out_specs=[
            pl.BlockSpec((Q, WIDE2), lambda i: (0, i)),
            pl.BlockSpec((N, WIDE2), lambda i: (0, i)),
            pl.BlockSpec((Q, LANES), lambda i: (0, 0)),
            pl.BlockSpec((Q, LANES), lambda i: (0, 0)),
            pl.BlockSpec((Q, N), lambda i: (0, i // per_group)),
            pl.BlockSpec((Q, N), lambda i: (0, i // per_group)),
        ],
        out_shape=[
            jax.ShapeDtypeStruct((Q, width), F32),
            jax.ShapeDtypeStruct((N, width), F32),
            jax.ShapeDtypeStruct((Q, LANES), F32),
            jax.ShapeDtypeStruct((Q, LANES), F32),
            jax.ShapeDtypeStruct((Q, groups * N), F32),
            jax.ShapeDtypeStruct((Q, groups * N), F32),
        ],
        scratch_shapes=[pltpu.VMEM((Q, 2 * Q), F32), pltpu.VMEM((Q, 2 * Q), F32), pltpu.VMEM((LANES, Q), F32)],
        cost_estimate=pl.CostEstimate(
            flops=16 * Q * Q * width, transcendentals=Q * Q * width // HEAD, bytes_accessed=14 * Q * width
        ),
    )(fhi, flo, col, row, mask, rows, x, g, far, b, c, far_small)


def finish_kernel(
    first, per_group, stages, last_ctx, weight_ref, khi_ref, klo_ref, ratio_ref, rate_ref, down_ref, cc_ref, r_ref, prev_ref, rows_ref,
    x_ref, g_ref, p_ref, tf_ref, b_ref, c_ref, gbi_ref, gci_ref, *refs,
):
    own_refs, other_refs = refs[:stages], refs[stages : 2 * stages]
    gi_ref, gb_ref, gc_ref, gs_ref, acc_ref, ab_ref, ac_ref = refs[-7:]
    i = pl.program_id(0)
    ctx = lax.axis_index("ctx")
    core = ctx % 2
    chip = ctx // 2
    low_edge = jnp.where(chip == 0, 0, 1)
    high_edge = jnp.where(chip == last_ctx // 2, 0, 1)
    weight = weight_ref[0, 0]

    @pl.when(i == 0)
    def _():
        acc_ref[...] = jnp.zeros_like(acc_ref)

    @pl.when(i % per_group == 0)
    def _():
        ab_ref[...] = jnp.zeros_like(ab_ref)
        ac_ref[...] = jnp.zeros_like(ac_ref)

    sel = head_selector((first + i) * (WIDE3 // HEAD), WIDE3)
    wide = nn(khi_ref[...], sel) + nn(klo_ref[...], sel)
    behind, before = wide[:Q], wide[Q:]
    shape = (N, WIDE3)
    sub = iota(shape, 0)
    carried, other = own_refs[0][...].astype(F32), other_refs[0][...].astype(F32)
    for k in range(1, stages):
        carried = carried + own_refs[k][...].astype(F32)
        other = other + other_refs[k][...].astype(F32)
    own_edge = jnp.where(core == 1, low_edge, high_edge)
    other_edge = jnp.where(core == 1, high_edge, low_edge)
    carried = jnp.where(sub < own_edge * N, carried, 0.0)
    other = jnp.where(sub < other_edge * N, other, 0.0)
    own = tf_ref[...] + rows_ref[0:1, :] * carried
    forward = forward_role(shape)
    state = jnp.where(forward, own, other)
    flow = jnp.where(forward, other, own)
    state_h, state_l = split(state)
    flow_h, flow_l = split(flow)
    b, c = b_ref[...], c_ref[...]
    x = x_ref[...].astype(F32)
    g = g_ref[...].astype(F32) * before
    reached = behind * (nn(b, flow_h) + nn(b, flow_l))
    gi_ref[...] = (weight * (p_ref[...] + reached)).astype(BF16)
    entered = g * (nn(c, state_h) + nn(c, state_l))
    g_h, g_l = split(g)
    x_h, x_l = split(x * behind)
    ab_ref[...] += nt(x_h, flow_h) + nt(x_h, flow_l) + nt(x_l, flow_h)
    ac_ref[...] += nt(g_h, state_h) + nt(g_h, state_l) + nt(g_l, state_h)
    through = jnp.sum((state * flow).reshape(N // 16, 16, WIDE3), axis=0)
    red_h, red_l = split(jnp.concatenate([x * reached, entered, through], axis=0))
    acc_ref[...] += nt(red_h, sel) + nt(red_l, sel)

    @pl.when(i % per_group == per_group - 1)
    def _():
        gb_ref[...] = (weight * (gbi_ref[...] + ab_ref[...])).astype(BF16)
        gc_ref[...] = (weight * (gci_ref[...] + ac_ref[...])).astype(BF16)

    @pl.when(i == pl.num_programs(0) - 1)
    def _():
        leaving, entering = acc_ref[:Q, :], acc_ref[Q : 2 * Q, :]
        passing = jnp.sum(acc_ref[2 * Q :, :], axis=0, keepdims=True) * down_ref[0:1, :]
        upper = (iota((Q, Q), 0) <= iota((Q, Q), 1)).astype(F32)
        inside = r_ref[...] + entering - cc_ref[...] - leaving
        decay = jnp.dot(upper, inside, precision=HIGHEST, preferred_element_type=F32)
        decay = decay + (passing + jnp.sum(leaving, axis=0, keepdims=True))
        steps = (cc_ref[...] + leaving) * ratio_ref[...] + rate_ref[...] * decay
        gs_ref[...] = prev_ref[...] + weight * steps


def finish(chunk, width, group_width, last_ctx, weight, tables, cc, r, prev, rows, x, g, p, tf, b, c, gbi, gci, own, other, partial):
    khi, klo, ratio, rate, down = tables
    steps = width // WIDE3
    first = chunk * steps
    per_group = group_width // WIDE3
    stages = len(own)
    whole = lambda a: pl.BlockSpec(a.shape, lambda i: (0, 0))
    local = pl.BlockSpec((Q, WIDE3), lambda i: (0, i))
    spread = pl.BlockSpec((Q, WIDE3), lambda i: (0, first + i))
    group = pl.BlockSpec((Q, N), lambda i: (0, (first + i) // per_group))
    inner = pl.BlockSpec((Q, N), lambda i: (0, i // per_group))
    operands = [weight, khi, klo, ratio, rate, down, cc, r, prev, rows, x, g, p, tf, b, c, gbi, gci, *own, *other]
    specs = [
        pl.BlockSpec(memory_space=pltpu.SMEM),
        whole(khi), whole(klo), whole(ratio), whole(rate), whole(down), whole(cc), whole(r), whole(prev),
        pl.BlockSpec((16, WIDE3), lambda i: (0, i)),
        spread, spread, local, local, group, group, inner, inner,
    ] + [local] * (2 * stages)
    aliases = {}
    if partial is not None:
        aliases = {len(operands) + k: k for k in range(3)}
        operands += list(partial)
        specs += [pl.BlockSpec(memory_space=pl.ANY)] * 3
    return pl.pallas_call(
        functools.partial(finish_kernel, first, per_group, stages, last_ctx),
        name="finish",
        grid=(steps,),
        in_specs=specs,
        out_specs=[spread, group, group, pl.BlockSpec((Q, LANES), lambda i: (0, 0))],
        out_shape=[
            jax.ShapeDtypeStruct(x.shape, BF16),
            jax.ShapeDtypeStruct(b.shape, BF16),
            jax.ShapeDtypeStruct(c.shape, BF16),
            jax.ShapeDtypeStruct((Q, LANES), F32),
        ],
        scratch_shapes=[pltpu.VMEM((2 * Q + 16, LANES), F32), pltpu.VMEM((Q, N), F32), pltpu.VMEM((Q, N), F32)],
        input_output_aliases=aliases,
        cost_estimate=pl.CostEstimate(flops=24 * N * Q * width, transcendentals=0, bytes_accessed=20 * Q * width),
    )(*operands)


def local(inputs, out_grad, b_matrix, c_matrix, step_raw, hidden, log_rates, step_bias, skip_head_gain, doc_lengths, counts):
    ctx_size, dp_size = lax.axis_size("ctx"), lax.axis_size("dp")
    chips = ctx_size // 2
    tokens, model = inputs.shape
    groups = b_matrix.shape[1] // N
    group_width = model // groups
    width = model // CHUNKS
    stages = max(1, chips // 2)
    ctx = lax.axis_index("ctx")
    dp = lax.axis_index("dp")
    core = ctx % 2
    chip = ctx // 2

    def swap(value):
        return lax.ppermute(value, "ctx", [(k, k ^ 1) for k in range(ctx_size)])

    chain_pairs = []
    for z in range(chips):
        chain_pairs.append((2 * z + 1, 2 * z + 3 if z < chips - 1 else 2 * z))
        chain_pairs.append((2 * z, 2 * z - 2 if z > 0 else 1))

    def chain(value):
        return lax.ppermute(value, "ctx", chain_pairs)

    def across(value, m):
        return lax.ppermute(value, "dp", [(k, k ^ m) for k in range(dp_size)])

    def along(value, m):
        return lax.ppermute(value, "ctx", [(k, k ^ (2 * m)) for k in range(ctx_size)])

    first_core = core == 0
    far_small = swap(jnp.concatenate([jnp.where(first_core, b_matrix, c_matrix), step_raw], axis=1))
    cuts = [slice(k * width, (k + 1) * width) for k in range(CHUNKS)]
    far = [swap(jnp.where(first_core, inputs[:, cut], out_grad[:, cut])) for cut in cuts]
    row = lambda a: a.reshape(1, -1)
    whi, wlo, fhi, flo, col, srow, mask, khi, klo, ratio, rate, down = prep(
        doc_lengths, step_raw, far_small, row(log_rates), row(step_bias), row(skip_head_gain), groups
    )
    formed = [
        chip_state(k, width, group_width, whi, wlo, inputs, out_grad, far[k], b_matrix, c_matrix, far_small)
        for k in range(CHUNKS)
    ]

    inner = jnp.where(first_core, chip < chips - 1, chip > 0)
    sending = [state for state, _ in formed]
    own = [[] for _ in range(CHUNKS)]
    other = [[] for _ in range(CHUNKS)]
    for stage in range(stages):
        for k in range(CHUNKS):
            arrived = chain(sending[k])
            own[k].append(arrived)
            other[k].append(swap(arrived))
            if stage < stages - 1:
                scale = formed[k][1][1:2, :]
                sending[k] = jnp.where(inner, arrived.astype(F32) * scale, 0.0).astype(BF16)

    count = counts.astype(F32)
    total = count
    m = 1
    while m < dp_size:
        total = total + across(total, m)
        m *= 2
    weight = (count * dp_size / total).reshape(1, 1)

    columns = model // dp_size
    cut_of = lambda index: lax.dynamic_slice_in_dim(hidden, index * columns, columns, 1)
    hidden_all = jnp.concatenate([cut_of(dp)] + [across(cut_of(dp ^ m), m) for m in range(1, dp_size)], axis=0)

    blocks = [
        within_block(
            k, width, group_width, fhi, flo, col, srow, mask, formed[k][1], inputs, out_grad, far[k], b_matrix, c_matrix, far_small
        )
        for k in range(CHUNKS)
    ]
    partial = None
    grad_steps = jnp.zeros((tokens, LANES), F32)
    for k in range(CHUNKS):
        p, tf, cc, r, gbi, gci = blocks[k]
        *partial, grad_steps = finish(
            k, width, group_width, ctx_size - 1, weight, (khi, klo, ratio, rate, down), cc, r, grad_steps, formed[k][1],
            inputs, out_grad, p, tf, b_matrix, c_matrix, gbi, gci, own[k], other[k], partial,
        )
    grad_inputs, grad_b, grad_c = partial
    grad_raw = grad_steps.astype(BF16)

    steps_all = jnp.concatenate([grad_raw] + [across(grad_raw, m) for m in range(1, dp_size)], axis=0)
    part = lax.dot_general(hidden_all, steps_all, (((0,), (0,)), ((), ())), preferred_element_type=F32)
    part = part.reshape(chips, 2, columns // ctx_size, LANES)
    pick = lambda index: lax.dynamic_index_in_dim(part, index, 1, keepdims=False)
    part = pick(core) + swap(pick(1 - core))
    piece = lambda index: lax.dynamic_index_in_dim(part, index, 0, keepdims=False)
    grad_weight = piece(chip)
    for m in range(1, chips):
        grad_weight = grad_weight + along(piece(chip ^ m), m)
    scaling = 1.0 / math.sqrt(dp_size * ctx_size * tokens)
    return (grad_inputs, grad_b, grad_c, grad_raw, grad_weight * scaling)


def solution(mesh):
    rows = P(("dp", "ctx"), None)
    return jax.shard_map(
        local,
        mesh=mesh,
        in_specs=(rows, rows, rows, rows, rows, rows, P(), P(), P(), P("dp", None), P("dp")),
        out_specs=(rows, rows, rows, rows, rows),
        check_vma=False,
    )
```
